256 devices in a mesh: leaf: 16 (over z, core), row: 4 (over x), col: 4 (over y).
Axes of the slice: x: 4, y: 4, z: 8, core: 2. Of those that a mesh axis runs over, the one named last changes fastest.
Arguments:
- rhs_leaf: bfloat16 [16, 8, 64, 2048], P('leaf', None, None, 'col'), may hold values from -6 to 6
- dinv_leaf: bfloat16 [16, 8, 2048, 2048], P('leaf', None, 'row', 'col'), as said below
- panel_leaf: bfloat16 [16, 8, 1024, 2048], P('leaf', None, 'col', 'row'), may hold values from -0.0234375 to 0.0234375
- counts: int32 [16, 8], P('leaf'), may hold values from 256 to 2048, as said below
- row_index: int32 [16, 8, 1024], P('leaf'), may hold values from 0 to 4095, as said below
- rhs_root: bfloat16 [64, 4096], P(None, 'col'), may hold values from -6 to 6
- dinv_root: bfloat16 [4096, 4096], P(('leaf', 'row')), as said below
Outputs:
- y_leaf: bfloat16 [16, 8, 64, 2048], P('leaf', None, None, 'row')
- y_root: bfloat16 [64, 4096], P(None, ('leaf', 'row'))
The draws below stay inside these ranges and needn't reach their ends.
Inputs may be any that keep to these rules, and one draw needn't show every extreme that they name: `counts`: each subtree supernode has at least 256 columns; at least one supernode of every draw has all 2048. `row_index`: within one supernode the 1024 entries are distinct and increasing. `dinv_leaf`: each [2048, 2048] block is lower triangular with a nonzero diagonal. `dinv_root`: lower triangular with a nonzero diagonal.
All inputs are finite; a program needn't handle non-finite values.
Results may differ from the reference program's by a relative error of at most 0.0053.
Values may be sent and summed in bfloat16 or wider, within the bound.
A program may use at most 64 MiB of HBM per device.

```python
import jax
import jax.numpy as jnp
from jax import lax

NRHS = 64
SA = 2048
RA = 1024
ST = 4096
KS = 8
GROUPS = 16
N_LEAF = 16


def lower_inverse(key, shape, order):
    first, second = jax.random.split(key)
    spread = jax.random.normal(first, shape, jnp.float32)
    diagonal = jax.random.uniform(second, shape[:-1], jnp.float32, 0.9, 1.3)
    lower = jnp.tril(spread * (0.6 / order ** 0.5), -1)
    eye = jnp.eye(order, dtype=jnp.float32)
    return lower + eye * diagonal[..., None]


def draw_dinv_leaf(key, part):
    return lower_inverse(jax.random.fold_in(key, 11), (GROUPS, KS, SA, SA), SA).astype(jnp.bfloat16)


def draw_dinv_root(key, part):
    return lower_inverse(jax.random.fold_in(key, 13), (ST, ST), ST).astype(jnp.bfloat16)


def draw_counts(key, part):
    first = jax.random.fold_in(key, 17)
    second = jax.random.fold_in(key, 19)
    values = jax.random.randint(first, (GROUPS * KS,), SA // 8, SA + 1)
    where = jax.random.randint(second, (), 0, GROUPS * KS)
    values = values.at[where].set(SA)
    return values.reshape(GROUPS, KS).astype(jnp.int32)


def draw_row_index(key, part):
    keys = jax.random.split(jax.random.fold_in(key, 23), GROUPS * KS)

    def pick(single):
        return jnp.sort(jax.random.permutation(single, ST)[:RA])
    chosen = jax.vmap(pick)(keys)
    return chosen.reshape(GROUPS, KS, RA).astype(jnp.int32)


def steps_of(rng, shape, cuts, smallest, high):
    def one(dim, parts):
        steps = jax.random.uniform(jax.random.fold_in(jax.random.fold_in(rng, 6), dim), (parts,), jnp.float32, smallest / len(cuts), high / len(cuts))
        return jnp.repeat(jnp.exp(steps), shape[dim] // parts).reshape((-1,) + (1,) * (len(shape) - dim - 1))

    gain = one(*cuts[0])
    for cut in cuts[1:]:
        gain = gain * one(*cut)
    return gain


def noise(own_key, shape, width, reach, cuts=(), kind=jnp.bfloat16):
    drawn = width * jax.random.normal(own_key, shape, jnp.float32)
    if cuts:
        drawn = drawn * steps_of(own_key, shape, cuts, -0.22, 0.18)
    return jnp.clip(drawn, -reach, reach).astype(kind)


def setup_inputs(seed: int = 0) -> dict:
    splits = jax.random.split(jax.random.key(seed), 8)
    return {
        "rhs_leaf": noise(splits[0], (GROUPS, KS, NRHS, SA), 1.0, 6.0, ((0, 16), (3, 4))),
        "dinv_leaf": draw_dinv_leaf(jax.random.fold_in(splits[7], 71), 0),
        "panel_leaf": noise(splits[2], (GROUPS, KS, RA, SA), (SA * N_LEAF * KS * RA // ST) ** -0.5, 0.0234375, ((0, 16), (2, 4), (3, 4))),
        "counts": draw_counts(jax.random.fold_in(splits[7], 71), 0),
        "row_index": draw_row_index(jax.random.fold_in(splits[7], 71), 0),
        "rhs_root": noise(splits[5], (NRHS, ST), 1.0, 6.0, ((1, 4),)),
        "dinv_root": draw_dinv_root(jax.random.fold_in(splits[7], 71), 0),
    }


def reference(rhs_leaf, dinv_leaf, panel_leaf, counts, row_index, rhs_root, dinv_root):
    slots = lax.iota(jnp.int32, SA)
    flat_rhs = rhs_leaf.reshape(GROUPS * KS, NRHS, SA)
    flat_inv = dinv_leaf.reshape(GROUPS * KS, SA, SA)
    flat_panel = panel_leaf.reshape(GROUPS * KS, RA, SA)
    flat_count = counts.reshape(GROUPS * KS).astype(jnp.int32)
    flat_rows = row_index.reshape(GROUPS * KS, RA).astype(jnp.int32)

    def one_node(total, items):
        right, inverse, panel, count, targets = items
        live = slots[None, :] < count
        masked = jnp.where(live, right, jnp.zeros((), jnp.bfloat16))
        solved = jnp.dot(masked, inverse.T, preferred_element_type=jnp.float32)
        solved = jnp.where(live, solved, jnp.zeros((), jnp.float32)).astype(jnp.bfloat16)
        update = jnp.dot(solved, panel.T, preferred_element_type=jnp.float32)
        total = total.at[:, targets].add(update)
        return total, solved

    start = jnp.zeros((NRHS, ST), jnp.float32)
    gathered, solved_all = lax.scan(one_node, start, (flat_rhs, flat_inv, flat_panel, flat_count, flat_rows))
    reduced = (rhs_root.astype(jnp.float32) - gathered).astype(jnp.bfloat16)
    y_root = jnp.dot(reduced, dinv_root.T, preferred_element_type=jnp.float32).astype(jnp.bfloat16)
    return solved_all.reshape(GROUPS, KS, NRHS, SA), y_root
```

```python
import jax
import jax.numpy as jnp
from jax import lax
from jax.experimental import pallas as pl
from jax.experimental.pallas import tpu as pltpu
from jax.sharding import PartitionSpec as P

BF16 = jnp.bfloat16
F32 = jnp.float32
MESH = pl.DeviceIdType.MESH
NODES, B, WC, PR, ROOT = 8, 64, 512, 256, 4096
TILE = 512


def dot_nt(a, b):
    return lax.dot_general(a, b, (((1,), (1,)), ((), ())), preferred_element_type=F32)


def body(counts, rhs_h, dinv_h, panel_h, rows_h, rroot_h, droot_h, yleaf_h, yroot_o,
         rhs, dinv, panel, rows, rroot, droot, s1, r1, s2, r2, y, hot, upd, acc,
         cs, cr, zs, zr, red, part, in_sem, s1_s, s1_r, s2_s, s2_r, y_sem,
         c_s, c_r, z_s, z_r, g_s, g_r, p_s, p_r):
    leaf, r, c = lax.axis_index("leaf"), lax.axis_index("row"), lax.axis_index("col")
    z, k = leaf // 2, leaf % 2
    near = c + 1 - 2 * (c % 2)
    far = 3 - c

    def load(src, dst, i):
        copy = pltpu.make_async_copy(src, dst, in_sem.at[i])
        copy.start()
        return copy

    order = [s for i in range(NODES // 2) for s in (i, i + NODES // 2)]
    loads = {}
    loads["rhs"] = load(rhs_h.at[0], rhs, 0)
    for s in order:
        loads["d", s] = load(dinv_h.at[0, s], dinv.at[s], 1 + s)
    cut = pl.multiple_of(c * PR, PR)
    loads["rows"] = load(rows_h.at[0, :, pl.ds(cut, PR)], rows, 17)
    for s in order:
        loads["p", s] = load(panel_h.at[0, s], panel.at[s], 9 + s)
    loads["rroot"] = load(rroot_h, rroot, 18)
    cut = pl.multiple_of(c * 1024, 1024)
    loads["droot"] = load(droot_h.at[:, pl.ds(cut, 1024)], droot, 19)

    def plane(dk, dr, dc):
        return (z * 2 + (k + dk) % 2, (r + dr) % 4, (c + dc) % 4)

    shifts = [(dk, dr, dc) for dc in (2, 1, 3, 0) for dr in (2, 1, 3, 0) for dk in (1, 0)]
    barrier = pltpu.get_barrier_semaphore()
    for shift in shifts[:-1]:
        pl.semaphore_signal(barrier, inc=1, device_id=plane(*shift), device_id_type=MESH)
    for dz in range(1, 8):
        pl.semaphore_signal(barrier, inc=1, device_id=(((z + dz) % 8) * 2 + k, r, c), device_id_type=MESH)
    pl.semaphore_wait(barrier, 38)

    def remote(src, dst, ss, rs, where):
        copy = pltpu.make_async_remote_copy(
            src_ref=src, dst_ref=dst, send_sem=ss, recv_sem=rs, device_id=where, device_id_type=MESH)
        copy.start()
        return copy

    lane = lax.broadcasted_iota(jnp.int32, (B, WC), 1)
    sends = []
    first, second = {}, {}
    loads["rhs"].wait()
    for s in order:
        loads["d", s].wait()
        masked = jnp.where(lane + c * WC < counts[0, s], rhs[s].astype(F32), 0.0).astype(BF16)
        s1[s] = dot_nt(masked, dinv[s]).astype(BF16)
        to = near if s < NODES // 2 else far
        first[s] = remote(s1.at[s], r1.at[s], s1_s.at[s], s1_r.at[s], (leaf, r, to))
    loads["rows"].wait()
    for i in range(NODES // 2):
        low = rows[i:i + 1, :]
        high = rows[i + NODES // 2:i + NODES // 2 + 1, :]

        def make(t, _, i=i, low=low, high=high):
            at = lax.broadcasted_iota(jnp.int32, (TILE, PR), 0) + t * TILE
            span = pl.ds(pl.multiple_of(t * TILE, TILE), TILE)
            hot[i, span, 0:PR] = jnp.where(at == low, 1.0, 0.0).astype(BF16)
            hot[i, span, PR:2 * PR] = jnp.where(at == high, 1.0, 0.0).astype(BF16)
            return 0

        lax.fori_loop(0, ROOT // TILE, make, 0)
        for s in (i, i + NODES // 2):
            first[s].wait_recv()
            s2[s] = (s1[s].astype(F32) + r1[s].astype(F32)).astype(BF16)
            to = far if s < NODES // 2 else near
            second[s] = remote(s2.at[s], r2.at[s], s2_s.at[s], s2_r.at[s], (leaf, r, to))
    outs = []
    for i in range(NODES // 2):
        for h, s in enumerate((i, i + NODES // 2)):
            second[s].wait_recv()
            total = s2[s].astype(F32) + r2[s].astype(F32)
            solved = jnp.where(lane + r * WC < counts[0, s], total, 0.0).astype(BF16)
            y[s] = solved
            out = pltpu.make_async_copy(y.at[s], yleaf_h.at[0, s], y_sem.at[s])
            out.start()
            outs.append(out)
            loads["p", s].wait()
            upd[:, h * PR:(h + 1) * PR] = dot_nt(solved, panel[s]).astype(BF16)
        if i < NODES // 2 - 1:

            def add(t, _, i=i):
                span = pl.ds(pl.multiple_of(t * TILE, TILE), TILE)
                got = dot_nt(upd[...], hot[i, span, :])
                acc[t] = got if i == 0 else acc[t] + got
                return 0

            lax.fori_loop(0, ROOT // TILE, add, 0)
        else:
            pieces = {}
            for dc in (2, 1, 3, 0):
                cb = (c + dc) % 4
                for half in range(2):
                    t = cb * 2 + half
                    span = pl.ds(pl.multiple_of(t * TILE, TILE), TILE)
                    tile = (acc[t] + dot_nt(upd[...], hot[i, span, :])).astype(BF16)
                    for q in range(4):
                        cs[cb * 8 + half * 4 + q] = tile[:, q * 128:(q + 1) * 128]
                for dr in (2, 1, 3, 0):
                    for dk in (1, 0):
                        if dc == 0 and dr == 0 and dk == 0:
                            continue
                        kb, rb = (k + dk) % 2, (r + dr) % 4
                        j = dc * 8 + dr * 2 + dk
                        pieces[j] = remote(cs.at[cb * 8 + rb * 2 + kb], cr.at[j], c_s.at[j], c_r.at[j],
                                           (z * 2 + kb, rb, cb))
    mine = r * 2 + k
    total = cs[c * 8 + mine].astype(F32)
    for j in pieces:
        pieces[j].wait_recv()
        total = total + cr[j].astype(F32)
    zs[...] = total.astype(BF16)
    zcopies = []
    for dz in (4, 3, 5, 2, 6, 1, 7):
        zcopies.append(remote(zs, zr.at[dz], z_s.at[dz], z_r.at[dz], (((z + dz) % 8) * 2 + k, r, c)))
    loads["rroot"].wait()
    total = rroot[:, pl.ds(pl.multiple_of(mine * 128, 128), 128)].astype(F32) - zs[...].astype(F32)
    for dz, copy in zip((4, 3, 5, 2, 6, 1, 7), zcopies):
        copy.wait_recv()
        total = total - zr[dz].astype(F32)
    red[mine] = total.astype(BF16)
    gathers = []
    for dr in (2, 1, 3, 0):
        for dk in (1, 0):
            if dr == 0 and dk == 0:
                continue
            j = dr * 2 + dk
            gathers.append(remote(red.at[mine], red.at[mine], g_s.at[j], g_r.at[j], plane(dk, dr, 0)))
    loads["droot"].wait()
    for copy in gathers:
        copy.wait_recv()
    whole = dot_nt(red[0], droot[:, 0:128])
    for q in range(1, 8):
        whole = whole + dot_nt(red[q], droot[:, q * 128:(q + 1) * 128])
    part[c] = whole
    shares = []
    for dc in (2, 1, 3):
        shares.append(remote(part.at[c], part.at[c], p_s.at[dc], p_r.at[dc], (leaf, r, (c + dc) % 4)))
    for copy in shares:
        copy.wait_recv()
    yroot_o[...] = (((part[0] + part[1]) + part[2]) + part[3]).astype(BF16)
    for copies in (first.values(), second.values(), pieces.values(), zcopies, gathers, shares):
        for copy in copies:
            copy.wait_send()
    for out in outs:
        out.wait()


def local(rhs_leaf, dinv_leaf, panel_leaf, counts, row_index, rhs_root, dinv_root):
    anywhere = pl.BlockSpec(memory_space=pl.ANY)
    dma = pltpu.SemaphoreType.DMA
    return pl.pallas_call(
        body,
        out_shape=(jax.ShapeDtypeStruct((1, NODES, B, WC), BF16), jax.ShapeDtypeStruct((B, 64), BF16)),
        in_specs=[pl.BlockSpec(memory_space=pltpu.SMEM)] + [anywhere] * 6,
        out_specs=(anywhere, pl.BlockSpec(memory_space=pltpu.VMEM)),
        scratch_shapes=[
            pltpu.VMEM((NODES, B, WC), BF16),
            pltpu.VMEM((NODES, WC, WC), BF16),
            pltpu.VMEM((NODES, PR, WC), BF16),
            pltpu.VMEM((NODES, PR), jnp.int32),
            pltpu.VMEM((B, 1024), BF16),
            pltpu.VMEM((64, 1024), BF16),
            pltpu.VMEM((NODES, B, WC), BF16),
            pltpu.VMEM((NODES, B, WC), BF16),
            pltpu.VMEM((NODES, B, WC), BF16),
            pltpu.VMEM((NODES, B, WC), BF16),
            pltpu.VMEM((NODES, B, WC), BF16),
            pltpu.VMEM((NODES // 2, ROOT, 2 * PR), BF16),
            pltpu.VMEM((B, 2 * PR), BF16),
            pltpu.VMEM((ROOT // TILE, B, TILE), F32),
            pltpu.VMEM((32, B, 128), BF16),
            pltpu.VMEM((32, B, 128), BF16),
            pltpu.VMEM((B, 128), BF16),
            pltpu.VMEM((8, B, 128), BF16),
            pltpu.VMEM((8, B, 128), BF16),
            pltpu.VMEM((4, B, 64), F32),
            dma((20,)), dma((8,)), dma((8,)), dma((8,)), dma((8,)), dma((8,)),
            dma((32,)), dma((32,)), dma((8,)), dma((8,)), dma((8,)), dma((8,)), dma((4,)), dma((4,)),
        ],
        compiler_params=pltpu.CompilerParams(
            collective_id=0, has_side_effects=True, vmem_limit_bytes=60 * 1024 * 1024),
        name="substitute",
    )(counts, rhs_leaf, dinv_leaf, panel_leaf, row_index, rhs_root, dinv_root)


def solution(mesh):
    in_specs = (
        P("leaf", None, None, "col"),
        P("leaf", None, "row", "col"),
        P("leaf", None, "col", "row"),
        P("leaf", None),
        P("leaf", None, None),
        P(None, "col"),
        P(("leaf", "row"), None),
    )
    out_specs = (P("leaf", None, None, "row"), P(None, ("leaf", "row")))
    return jax.shard_map(local, mesh=mesh, in_specs=in_specs, out_specs=out_specs, check_vma=False)
```

```python
import jax
import jax.numpy as jnp
from jax import lax
from jax.experimental import pallas as pl
from jax.experimental.pallas import tpu as pltpu
from jax.sharding import PartitionSpec as P

BF16 = jnp.bfloat16
F32 = jnp.float32
MESH = pl.DeviceIdType.MESH
NODES, B, WC, PR, ROOT = 8, 64, 512, 256, 4096
TILE = 512


def dot_nn(a, b):
    return lax.dot_general(a, b, (((1,), (0,)), ((), ())), preferred_element_type=F32)


def dot_nt(a, b):
    return lax.dot_general(a, b, (((1,), (1,)), ((), ())), preferred_element_type=F32)


def body(counts, rhs_h, dinv_h, panel_h, rows_h, rroot_h, droot_h, yleaf_h, yroot_o,
         rhs, dinv, panel, rows, rroot, droot, s1, r1, s2, r2, y, hot, upd, acc,
         cs, cr, zs, zr, red, part, in_sem, s1_s, s1_r, s2_s, s2_r, y_sem,
         c_s, c_r, z_s, z_r, g_s, g_r, p_s, p_r, relay):
    leaf, r, c = lax.axis_index("leaf"), lax.axis_index("row"), lax.axis_index("col")
    z, k = leaf // 2, leaf % 2
    near = c + 1 - 2 * (c % 2)
    far = 3 - c

    def load(src, dst, i):
        copy = pltpu.make_async_copy(src, dst, in_sem.at[i])
        copy.start()
        return copy

    order = [s for i in range(NODES // 2) for s in (i, i + NODES // 2)]
    loads = {}
    loads["rhs"] = load(rhs_h.at[0], rhs, 0)
    for s in order:
        loads["d", s] = load(dinv_h.at[0, s], dinv.at[s], 1 + s)
    cut = pl.multiple_of(c * PR, PR)
    loads["rows"] = load(rows_h.at[0, :, pl.ds(cut, PR)], rows, 17)
    for s in order:
        loads["p", s] = load(panel_h.at[0, s], panel.at[s], 9 + s)
    loads["rroot"] = load(rroot_h, rroot, 18)
    cut = pl.multiple_of(c * 1024, 1024)
    loads["droot"] = load(droot_h.at[:, pl.ds(cut, 1024)], droot, 19)

    def plane(dk, dr, dc):
        return (z * 2 + (k + dk) % 2, (r + dr) % 4, (c + dc) % 4)

    line_y = [plane(0, 0, dc) for dc in (1, 2, 3)]
    line_x = [plane(0, dr, 0) for dr in (1, 2, 3)]
    line_z = [(((z + dz) % 8) * 2 + k, r, c) for dz in (1, 7)]
    pair = [plane(1, 0, 0)]
    barrier = pltpu.get_barrier_semaphore()
    for where in line_y + line_x + pair + line_z:
        pl.semaphore_signal(barrier, inc=1, device_id=where, device_id_type=MESH)

    def tell(i, peers):
        for where in peers:
            pl.semaphore_signal(relay.at[i], inc=1, device_id=where, device_id_type=MESH)

    def heard(i, count):
        pl.semaphore_wait(relay.at[i], count)

    def remote(src, dst, ss, rs, where):
        copy = pltpu.make_async_remote_copy(
            src_ref=src, dst_ref=dst, send_sem=ss, recv_sem=rs, device_id=where, device_id_type=MESH)
        copy.start()
        return copy

    lane = lax.broadcasted_iota(jnp.int32, (B, WC), 1)
    first, second = {}, {}
    loads["rhs"].wait()
    for s in order:
        loads["d", s].wait()
        masked = jnp.where(lane + c * WC < counts[0, s], rhs[s].astype(F32), 0.0).astype(BF16)
        s1[s] = dot_nt(masked, dinv[s]).astype(BF16)
        to = near if s < NODES // 2 else far
        if s == order[0]:
            pl.semaphore_wait(barrier, 9)
            tell(0, line_x)
            tell(2, line_z)
        first[s] = remote(s1.at[s], r1.at[s], s1_s.at[s], s1_r.at[s], (leaf, r, to))
    loads["rows"].wait()
    targets = jnp.transpose(rows[...])
    for i in range(NODES // 2):
        low = targets[:, i:i + 1]
        high = targets[:, i + NODES // 2:i + NODES // 2 + 1]

        def make(t, _, i=i, low=low, high=high):
            at = lax.broadcasted_iota(jnp.int32, (PR, TILE), 1) + t * TILE
            hot[i, t, 0:PR, :] = jnp.where(at == low, 1.0, 0.0).astype(BF16)
            hot[i, t, PR:2 * PR, :] = jnp.where(at == high, 1.0, 0.0).astype(BF16)
            return 0

        lax.fori_loop(0, ROOT // TILE, make, 0)
        for s in (i, i + NODES // 2):
            first[s].wait_recv()
            s2[s] = (s1[s].astype(F32) + r1[s].astype(F32)).astype(BF16)
            to = far if s < NODES // 2 else near
            second[s] = remote(s2.at[s], r2.at[s], s2_s.at[s], s2_r.at[s], (leaf, r, to))
        if i == 0:
            heard(0, 3)
            tell(1, pair)
        if i < 3:
            heard(2 + i, 2)
        if i < 2:
            tell(3 + i, line_z)
    outs = []
    for i in range(NODES // 2):
        for h, s in enumerate((i, i + NODES // 2)):
            second[s].wait_recv()
            total = s2[s].astype(F32) + r2[s].astype(F32)
            solved = jnp.where(lane + r * WC < counts[0, s], total, 0.0).astype(BF16)
            y[s] = solved
            out = pltpu.make_async_copy(y.at[s], yleaf_h.at[0, s], y_sem.at[s])
            out.start()
            outs.append(out)
            loads["p", s].wait()
            upd[:, h * PR:(h + 1) * PR] = dot_nt(solved, panel[s]).astype(BF16)
        if i < NODES // 2 - 1:
            for t in range(ROOT // TILE):
                got = dot_nn(upd[...], hot[i, t])
                acc[t] = got if i == 0 else acc[t] + got
        else:
            heard(1, 1)
            pieces = {}
            for dc in (2, 1, 3, 0):
                cb = (c + dc) % 4
                for half in range(2):
                    t = cb * 2 + half
                    tile = (acc[t] + dot_nn(upd[...], hot[i, t])).astype(BF16)
                    for q in range(4):
                        cs[cb * 8 + half * 4 + q] = tile[:, q * 128:(q + 1) * 128]
                for dr in (2, 1, 3, 0):
                    for dk in (1, 0):
                        if dc == 0 and dr == 0 and dk == 0:
                            continue
                        kb, rb = (k + dk) % 2, (r + dr) % 4
                        j = dc * 8 + dr * 2 + dk
                        pieces[j] = remote(cs.at[cb * 8 + rb * 2 + kb], cr.at[j], c_s.at[j], c_r.at[j],
                                           (z * 2 + kb, rb, cb))
    mine = r * 2 + k
    total = cs[c * 8 + mine].astype(F32)
    for j in pieces:
        pieces[j].wait_recv()
        total = total + cr[j].astype(F32)
    zs[...] = total.astype(BF16)
    zcopies = []
    for dz in (4, 3, 5, 2, 6, 1, 7):
        zcopies.append(remote(zs, zr.at[dz], z_s.at[dz], z_r.at[dz], (((z + dz) % 8) * 2 + k, r, c)))
    loads["rroot"].wait()
    total = rroot[:, pl.ds(pl.multiple_of(mine * 128, 128), 128)].astype(F32) - zs[...].astype(F32)
    for dz, copy in zip((4, 3, 5, 2, 6, 1, 7), zcopies):
        copy.wait_recv()
        total = total - zr[dz].astype(F32)
    lanes = pl.ds(pl.multiple_of(k * 128, 128), 128)
    red[r, :, lanes] = total.astype(BF16)
    gathers = {}
    for dr in (2, 1, 3, 0):
        for dk in (1, 0):
            if dr == 0 and dk == 0:
                continue
            j = dr * 2 + dk
            spot = red.at[r, :, lanes]
            gathers[j] = remote(spot, spot, g_s.at[j], g_r.at[j], plane(dk, dr, 0))
    loads["droot"].wait()
    whole = jnp.zeros((B, 64), F32)
    for dr in (0, 1, 3, 2):
        for dk in (1, 0):
            if dr or dk:
                gathers[dr * 2 + dk].wait_recv()
        rb = (r + 4 - dr) % 4
        whole = whole + dot_nt(red[rb], droot[:, pl.ds(pl.multiple_of(rb * 256, 256), 256)])
    half = B // 2
    part[c] = jnp.concatenate([whole[0:half], whole[half:B]], axis=1)
    shares = []
    for dc in (2, 1, 3):
        shares.append(remote(part.at[c], part.at[c], p_s.at[dc], p_r.at[dc], (leaf, r, (c + dc) % 4)))
    for copy in shares:
        copy.wait_recv()
    final = (((part[0] + part[1]) + part[2]) + part[3]).astype(BF16)
    yroot_o[0:half, :] = final[:, 0:64]
    yroot_o[half:B, :] = final[:, 64:128]
    for copies in (first.values(), second.values(), pieces.values(), zcopies, gathers.values(), shares):
        for copy in copies:
            copy.wait_send()
    for out in outs:
        out.wait()


def local(rhs_leaf, dinv_leaf, panel_leaf, counts, row_index, rhs_root, dinv_root):
    anywhere = pl.BlockSpec(memory_space=pl.ANY)
    dma = pltpu.SemaphoreType.DMA
    return pl.pallas_call(
        body,
        out_shape=(jax.ShapeDtypeStruct((1, NODES, B, WC), BF16), jax.ShapeDtypeStruct((B, 64), BF16)),
        in_specs=[pl.BlockSpec(memory_space=pltpu.SMEM)] + [anywhere] * 6,
        out_specs=(anywhere, pl.BlockSpec(memory_space=pltpu.VMEM)),
        scratch_shapes=[
            pltpu.VMEM((NODES, B, WC), BF16),
            pltpu.VMEM((NODES, WC, WC), BF16),
            pltpu.VMEM((NODES, PR, WC), BF16),
            pltpu.VMEM((NODES, PR), jnp.int32),
            pltpu.VMEM((B, 1024), BF16),
            pltpu.VMEM((64, 1024), BF16),
            pltpu.VMEM((NODES, B, WC), BF16),
            pltpu.VMEM((NODES, B, WC), BF16),
            pltpu.VMEM((NODES, B, WC), BF16),
            pltpu.VMEM((NODES, B, WC), BF16),
            pltpu.VMEM((NODES, B, WC), BF16),
            pltpu.VMEM((NODES // 2, ROOT // TILE, 2 * PR, TILE), BF16),
            pltpu.VMEM((B, 2 * PR), BF16),
            pltpu.VMEM((ROOT // TILE, B, TILE), F32),
            pltpu.VMEM((32, B, 128), BF16),
            pltpu.VMEM((32, B, 128), BF16),
            pltpu.VMEM((B, 128), BF16),
            pltpu.VMEM((8, B, 128), BF16),
            pltpu.VMEM((4, B, 256), BF16),
            pltpu.VMEM((4, B // 2, 128), F32),
            dma((20,)), dma((8,)), dma((8,)), dma((8,)), dma((8,)), dma((8,)),
            dma((32,)), dma((32,)), dma((8,)), dma((8,)), dma((8,)), dma((8,)), dma((4,)), dma((4,)),
            pltpu.SemaphoreType.REGULAR((5,)),
        ],
        compiler_params=pltpu.CompilerParams(
            collective_id=0, has_side_effects=True, vmem_limit_bytes=60 * 1024 * 1024),
        name="substitute",
    )(counts, rhs_leaf, dinv_leaf, panel_leaf, row_index, rhs_root, dinv_root)


def solution(mesh):
    in_specs = (
        P("leaf", None, None, "col"),
        P("leaf", None, "row", "col"),
        P("leaf", None, "col", "row"),
        P("leaf", None),
        P("leaf", None, None),
        P(None, "col"),
        P(("leaf", "row"), None),
    )
    out_specs = (P("leaf", None, None, "row"), P(None, ("leaf", "row")))
    return jax.shard_map(local, mesh=mesh, in_specs=in_specs, out_specs=out_specs, check_vma=False)
```

```python
import jax
import jax.numpy as jnp
from jax import lax
from jax.experimental import pallas as pl
from jax.experimental.pallas import tpu as pltpu
from jax.sharding import PartitionSpec as P

BF16 = jnp.bfloat16
F32 = jnp.float32
MESH = pl.DeviceIdType.MESH
NODES, B, WC, PR, ROOT = 8, 64, 512, 256, 4096
TILE = 512


def dot_nn(a, b):
    return lax.dot_general(a, b, (((1,), (0,)), ((), ())), preferred_element_type=F32)


def dot_nt(a, b):
    return lax.dot_general(a, b, (((1,), (1,)), ((), ())), preferred_element_type=F32)


def body(counts, rhs_h, dinv_h, panel_h, rows_h, rroot_h, droot_h, yleaf_h, yroot_o,
         rhs, dinv, panel, rows, rroot, droot, s1, r1, s2, r2, y, hot, upd, acc,
         cs, cr, zs, zr, red, root, in_sem, s1_s, s1_r, s2_s, s2_r, y_sem,
         c_s, c_r, z_s, z_r, g_s, g_r, relay):
    leaf, r, c = lax.axis_index("leaf"), lax.axis_index("row"), lax.axis_index("col")
    z, k = leaf // 2, leaf % 2
    near = c + 1 - 2 * (c % 2)
    far = 3 - c

    def load(src, dst, i):
        copy = pltpu.make_async_copy(src, dst, in_sem.at[i])
        copy.start()
        return copy

    order = [s for i in range(NODES // 2) for s in (i, i + NODES // 2)]
    loads = {}
    for s in order:
        loads["r", s] = load(rhs_h.at[0, s], rhs.at[s], 20 + s)
        loads["d", s] = load(dinv_h.at[0, s], dinv.at[s], 1 + s)
    cut = pl.multiple_of(c * PR, PR)
    loads["rows"] = load(rows_h.at[0, :, pl.ds(cut, PR)], rows, 17)
    for s in order:
        loads["p", s] = load(panel_h.at[0, s], panel.at[s], 9 + s)
    loads["rroot"] = load(rroot_h, rroot, 18)
    loads["droot"] = load(droot_h, droot, 19)

    def plane(dk, dr, dc):
        return (z * 2 + (k + dk) % 2, (r + dr) % 4, (c + dc) % 4)

    me = k * 16 + r * 4 + c
    group = c * 2 + k
    shifts = [(dk, dr, dc) for dc in (2, 1, 3, 0) for dr in (2, 1, 3, 0) for dk in (1, 0)]
    line_y = [plane(0, 0, dc) for dc in (1, 2, 3)]
    line_x = [plane(0, dr, 0) for dr in (1, 2, 3)]
    line_z = [(((z + dz) % 8) * 2 + k, r, c) for dz in (1, 7)]
    pair = [plane(1, 0, 0)]
    barrier = pltpu.get_barrier_semaphore()
    for where in line_y + line_x + pair + line_z:
        pl.semaphore_signal(barrier, inc=1, device_id=where, device_id_type=MESH)

    def tell(i, peers):
        for where in peers:
            pl.semaphore_signal(relay.at[i], inc=1, device_id=where, device_id_type=MESH)

    def heard(i, count):
        pl.semaphore_wait(relay.at[i], count)

    def describe(src, dst, ss, rs, where):
        return pltpu.make_async_remote_copy(
            src_ref=src, dst_ref=dst, send_sem=ss, recv_sem=rs, device_id=where, device_id_type=MESH)

    def remote(src, dst, ss, rs, where):
        copy = describe(src, dst, ss, rs, where)
        copy.start()
        return copy

    lane = lax.broadcasted_iota(jnp.int32, (B, WC), 1)
    first, second = {}, {}
    for s in order:
        loads["r", s].wait()
        loads["d", s].wait()
        masked = jnp.where(lane + c * WC < counts[0, s], rhs[s].astype(F32), 0.0).astype(BF16)
        s1[s] = dot_nt(masked, dinv[s]).astype(BF16)
        to = near if s < NODES // 2 else far
        if s == order[0]:
            pl.semaphore_wait(barrier, 9)
            tell(0, line_x)
            tell(2, line_z)
        first[s] = remote(s1.at[s], r1.at[s], s1_s.at[s], s1_r.at[s], (leaf, r, to))
    loads["rows"].wait()
    targets = jnp.transpose(rows[...])
    for i in range(NODES // 2):
        low = targets[:, i:i + 1]
        high = targets[:, i + NODES // 2:i + NODES // 2 + 1]

        def make(t, _, i=i, low=low, high=high):
            at = lax.broadcasted_iota(jnp.int32, (PR, TILE), 1) + t * TILE
            hot[i, t, 0:PR, :] = jnp.where(at == low, 1.0, 0.0).astype(BF16)
            hot[i, t, PR:2 * PR, :] = jnp.where(at == high, 1.0, 0.0).astype(BF16)
            return 0

        lax.fori_loop(0, ROOT // TILE, make, 0)
        for s in (i, i + NODES // 2):
            first[s].wait_recv()
            s2[s] = (s1[s].astype(F32) + r1[s].astype(F32)).astype(BF16)
            to = far if s < NODES // 2 else near
            second[s] = remote(s2.at[s], r2.at[s], s2_s.at[s], s2_r.at[s], (leaf, r, to))
        if i == 0:
            heard(0, 3)
            tell(1, pair)
        if i < 3:
            heard(2 + i, 2)
        if i < 2:
            tell(3 + i, line_z)
    outs = []
    for i in range(NODES // 2):
        for h, s in enumerate((i, i + NODES // 2)):
            second[s].wait_recv()
            total = s2[s].astype(F32) + r2[s].astype(F32)
            solved = jnp.where(lane + r * WC < counts[0, s], total, 0.0).astype(BF16)
            y[s] = solved
            out = pltpu.make_async_copy(y.at[s], yleaf_h.at[0, s], y_sem.at[s])
            out.start()
            outs.append(out)
            loads["p", s].wait()
            upd[:, h * PR:(h + 1) * PR] = dot_nt(solved, panel[s]).astype(BF16)
        if i < NODES // 2 - 1:
            for t in range(ROOT // TILE):
                got = dot_nn(upd[...], hot[i, t])
                acc[t] = got if i == 0 else acc[t] + got
        else:
            heard(1, 1)
            for t in range(8):
                tile = (acc[t] + dot_nn(upd[...], hot[i, t])).astype(BF16)
                for q in range(4):
                    cs[t * 4 + q] = tile[:, q * 128:(q + 1) * 128]
                for q in range(4):
                    owner = (t % 2) * 16 + q * 4 + t // 2

                    @pl.when(me == owner)
                    def _(p=t * 4 + q, owner=owner):
                        cr[owner] = cs[p]

                    @pl.when(me != owner)
                    def _(p=t * 4 + q, t=t, q=q):
                        remote(cs.at[p], cr.at[me], c_s.at[p], c_r.at[me], (z * 2 + t % 2, q, t // 2))

    total = jnp.zeros((B, 128), F32)
    for slot in range(32):

        @pl.when(me != slot)
        def _(slot=slot):
            describe(cs.at[0], cr.at[slot], c_s.at[0], c_r.at[slot], pair[0]).wait_recv()

        total = total + cr[slot].astype(F32)
    zs[...] = total.astype(BF16)

    def to_plane(to):
        return describe(zs, zr.at[z], z_s.at[to], z_r.at[z], (to * 2 + k, r, c))

    for to in range(8):

        @pl.when((to >= group) & (to != z))
        def _(to=to):
            to_plane(to).start()

    spot = red.at[group, :, pl.ds(pl.multiple_of(r * 128, 128), 128)]

    def to_peer(shift):
        j = shift[0] * 16 + shift[1] * 4 + shift[2]
        return describe(spot, spot, g_s.at[j], g_r.at[group * 4 + r], plane(*shift))

    loads["rroot"].wait()

    @pl.when(z >= group)
    def _():
        zr[z] = zs[...]
        total = rroot[:, pl.ds(pl.multiple_of((k * 4 + r) * 128, 128), 128)].astype(F32)
        for other in range(8):

            @pl.when(z != other)
            def _(other=other):
                describe(zs, zr.at[other], z_s.at[other], z_r.at[other], pair[0]).wait_recv()

        for other in range(8):
            total = total - zr[other].astype(F32)
        spot[...] = total.astype(BF16)
        for shift in shifts[:-1]:
            to_peer(shift).start()

    loads["droot"].wait()
    for g in range(8):

        @pl.when(z >= g)
        def _(g=g):
            for q in range(4):

                @pl.when((group != g) | (r != q))
                def _(q=q):
                    block = red.at[g, :, q * 128:(q + 1) * 128]
                    describe(block, block, g_s.at[0], g_r.at[g * 4 + q], pair[0]).wait_recv()

            share = dot_nt(red[g], droot[:, g * 512:(g + 1) * 512])
            root[...] = share if g == 0 else root[...] + share

    yroot_o[...] = root[...].astype(BF16)
    for t in range(8):
        for q in range(4):

            @pl.when(me != (t % 2) * 16 + q * 4 + t // 2)
            def _(p=t * 4 + q):
                describe(cs.at[p], cr.at[me], c_s.at[p], c_r.at[me], pair[0]).wait_send()

    for to in range(8):

        @pl.when((to >= group) & (to != z))
        def _(to=to):
            to_plane(to).wait_send()

    @pl.when(z >= group)
    def _():
        for shift in shifts[:-1]:
            to_peer(shift).wait_send()

    for copies in (first.values(), second.values()):
        for copy in copies:
            copy.wait_send()
    for out in outs:
        out.wait()


def store(y, root, y_out, root_out, y_v, root_v, sem):
    copies = [pltpu.make_async_copy(y.at[0, pl.ds(i * 2, 2)], y_v.at[pl.ds(i * 2, 2)], sem.at[i]) for i in range(4)]
    copies.append(pltpu.make_async_copy(root, root_v, sem.at[4]))
    outs = [pltpu.make_async_copy(y_v.at[pl.ds(i * 2, 2)], y_out.at[0, pl.ds(i * 2, 2)], sem.at[5 + i]) for i in range(4)]
    outs.append(pltpu.make_async_copy(root_v, root_out, sem.at[9]))
    for copy in copies:
        copy.start()
    for copy, out in zip(copies, outs):
        copy.wait()
        out.start()
    for out in outs:
        out.wait()


def local(rhs_leaf, dinv_leaf, panel_leaf, counts, row_index, rhs_root, dinv_root):
    anywhere = pl.BlockSpec(memory_space=pl.ANY)
    dma = pltpu.SemaphoreType.DMA
    y_leaf, y_root = pl.pallas_call(
        body,
        out_shape=(jax.ShapeDtypeStruct((1, NODES, B, WC), BF16), jax.ShapeDtypeStruct((B, 64), BF16)),
        in_specs=[pl.BlockSpec(memory_space=pltpu.SMEM)] + [anywhere] * 6,
        out_specs=(anywhere, pl.BlockSpec(memory_space=pltpu.VMEM)),
        scratch_shapes=[
            pltpu.VMEM((NODES, B, WC), BF16),
            pltpu.VMEM((NODES, WC, WC), BF16),
            pltpu.VMEM((NODES, PR, WC), BF16),
            pltpu.VMEM((NODES, PR), jnp.int32),
            pltpu.VMEM((B, 1024), BF16),
            pltpu.VMEM((64, ROOT), BF16),
            pltpu.VMEM((NODES, B, WC), BF16),
            pltpu.VMEM((NODES, B, WC), BF16),
            pltpu.VMEM((NODES, B, WC), BF16),
            pltpu.VMEM((NODES, B, WC), BF16),
            pltpu.VMEM((NODES, B, WC), BF16),
            pltpu.VMEM((NODES // 2, ROOT // TILE, 2 * PR, TILE), BF16),
            pltpu.VMEM((B, 2 * PR), BF16),
            pltpu.VMEM((ROOT // TILE, B, TILE), F32),
            pltpu.VMEM((32, B, 128), BF16),
            pltpu.VMEM((32, B, 128), BF16),
            pltpu.VMEM((B, 128), BF16),
            pltpu.VMEM((8, B, 128), BF16),
            pltpu.VMEM((8, B, 512), BF16),
            pltpu.VMEM((B, 64), F32),
            dma((28,)), dma((8,)), dma((8,)), dma((8,)), dma((8,)), dma((8,)),
            dma((32,)), dma((32,)), dma((8,)), dma((8,)), dma((32,)), dma((32,)),
            pltpu.SemaphoreType.REGULAR((5,)),
        ],
        compiler_params=pltpu.CompilerParams(
            collective_id=0, has_side_effects=True, vmem_limit_bytes=60 * 1024 * 1024),
        name="substitute",
    )(counts, rhs_leaf, dinv_leaf, panel_leaf, row_index, rhs_root, dinv_root)
    return pl.pallas_call(
        store,
        out_shape=(jax.ShapeDtypeStruct((1, NODES, B, WC), BF16), jax.ShapeDtypeStruct((B, 64), BF16)),
        in_specs=[anywhere] * 2,
        out_specs=(anywhere, anywhere),
        scratch_shapes=[pltpu.VMEM((NODES, B, WC), BF16), pltpu.VMEM((B, 64), BF16), dma((10,))],
        compiler_params=pltpu.CompilerParams(vmem_limit_bytes=60 * 1024 * 1024),
        name="store",
    )(y_leaf, y_root)


def solution(mesh):
    in_specs = (
        P("leaf", None, None, "col"),
        P("leaf", None, "row", "col"),
        P("leaf", None, "col", "row"),
        P("leaf", None),
        P("leaf", None, None),
        P(None, "col"),
        P(("leaf", "row"), None),
    )
    out_specs = (P("leaf", None, None, "row"), P(None, ("leaf", "row")))
    return jax.shard_map(local, mesh=mesh, in_specs=in_specs, out_specs=out_specs, check_vma=False)
```

```python
import jax
import jax.numpy as jnp
from jax import lax
from jax.experimental import pallas as pl
from jax.experimental.pallas import tpu as pltpu
from jax.sharding import PartitionSpec as P

BF16 = jnp.bfloat16
F32 = jnp.float32
MESH = pl.DeviceIdType.MESH
NODES, B, WC, PR, ROOT = 8, 64, 512, 256, 4096
TILE = 512


def dot_nn(a, b):
    return lax.dot_general(a, b, (((1,), (0,)), ((), ())), preferred_element_type=F32)


def dot_nt(a, b):
    return lax.dot_general(a, b, (((1,), (1,)), ((), ())), preferred_element_type=F32)


def body(counts_h, rhs_h, dinv_h, panel_h, rows_h, rroot_h, droot_h, yleaf_h, yroot_o,
         counts, rhs, dinv, panel, rows, rroot, droot, s1, r1, s2, r2, y, wanted, hot, upd, acc, give, take,
         cs, cr, zs, zr, red, root, in_sem, s1_s, s1_r, s2_s, s2_r, y_sem,
         c_s, c_r, z_s, z_r, g_s, g_r, u_s, u_r, relay):
    leaf, r, c = lax.axis_index("leaf"), lax.axis_index("row"), lax.axis_index("col")
    z, k = leaf // 2, leaf % 2
    near = c + 1 - 2 * (c % 2)
    far = 3 - c

    def load(src, dst, i):
        copy = pltpu.make_async_copy(src, dst, in_sem.at[i])
        copy.start()
        return copy

    order = [s for i in range(NODES // 2) for s in (i, i + NODES // 2)]
    loads = {}
    loads["counts"] = load(counts_h, counts, 0)
    for s in order:
        loads["r", s] = load(rhs_h.at[0, s], rhs.at[s], 20 + s)
        loads["d", s] = load(dinv_h.at[0, s], dinv.at[s], 1 + s)
    def plane(dk, dr, dc):
        return (z * 2 + (k + dk) % 2, (r + dr) % 4, (c + dc) % 4)

    spot16 = r * 4 + c
    group = c * 2 + k
    shifts = [(dk, dr, dc) for dc in (2, 1, 3, 0) for dr in (2, 1, 3, 0) for dk in (1, 0)]
    line_y = [plane(0, 0, dc) for dc in (1, 2, 3)]
    line_x = [plane(0, dr, 0) for dr in (1, 2, 3)]
    line_z = [(((z + dz) % 8) * 2 + k, r, c) for dz in (1, 7)]
    pair = [plane(1, 0, 0)]
    barrier = pltpu.get_barrier_semaphore()
    for where in line_y + line_x + pair + line_z:
        pl.semaphore_signal(barrier, inc=1, device_id=where, device_id_type=MESH)

    cut = pl.multiple_of(c * PR, PR)
    loads["rows"] = load(rows_h.at[0, :, pl.ds(cut, PR)], rows, 17)
    for s in order:
        loads["p", s] = load(panel_h.at[0, s], panel.at[s], 9 + s)
    loads["rroot"] = load(rroot_h, rroot, 18)
    loads["droot"] = load(droot_h, droot, 19)

    def tell(i, peers):
        for where in peers:
            pl.semaphore_signal(relay.at[i], inc=1, device_id=where, device_id_type=MESH)

    def heard(i, count):
        pl.semaphore_wait(relay.at[i], count)

    def describe(src, dst, ss, rs, where):
        return pltpu.make_async_remote_copy(
            src_ref=src, dst_ref=dst, send_sem=ss, recv_sem=rs, device_id=where, device_id_type=MESH)

    def remote(src, dst, ss, rs, where):
        copy = describe(src, dst, ss, rs, where)
        copy.start()
        return copy

    lane = lax.broadcasted_iota(jnp.int32, (B, WC), 1)
    first, second = {}, {}
    loads["counts"].wait()
    for i in range(NODES // 2):
        both = (i, i + NODES // 2)
        for s in both:
            loads["r", s].wait()
            loads["d", s].wait()
        for s in both:
            masked = jnp.where(lane + c * WC < counts[0, s], rhs[s].astype(F32), 0.0).astype(BF16)
            s1[s] = dot_nt(masked, dinv[s]).astype(BF16)
        if i == 0:
            pl.semaphore_wait(barrier, 9)
        for s, to in zip(both, (near, far)):
            first[s] = remote(s1.at[s], r1.at[s], s1_s.at[s], s1_r.at[s], (leaf, r, to))
        if i == 0:
            tell(0, line_x)
            tell(2, line_z)
    loads["rows"].wait()
    targets = jnp.transpose(rows[...])
    lanes = lax.broadcasted_iota(jnp.int32, (PR, 128), 1)
    for i in range(NODES // 2):
        for h in range(2):
            node = i + h * NODES // 2
            wanted[h] = jnp.broadcast_to(targets[:, node:node + 1], (PR, 128)) - lanes

        def make(t, _, i=i):
            for h in range(2):
                want = wanted[h]
                for q in range(4):
                    hot[i, t, h * PR:(h + 1) * PR, q * 128:(q + 1) * 128] = jnp.where(
                        want == t * TILE + q * 128, 1.0, 0.0).astype(BF16)
            return 0

        lax.fori_loop(0, ROOT // TILE, make, 0)
        both = (i, i + NODES // 2)
        for s in both:
            first[s].wait_recv()
        for s in both:
            s2[s] = (s1[s].astype(F32) + r1[s].astype(F32)).astype(BF16)
        for s, to in zip(both, (far, near)):
            second[s] = remote(s2.at[s], r2.at[s], s2_s.at[s], s2_r.at[s], (leaf, r, to))
        if i == 0:
            heard(0, 3)
            tell(1, pair)
        if i < 3:
            heard(2 + i, 2)
        if i < 2:
            tell(3 + i, line_z)
    for s in order:
        loads["p", s].wait()
    base = c // 2
    outs = []
    for i in range(NODES // 2):
        both = (i, i + NODES // 2)
        for s in both:
            second[s].wait_recv()
        for h, s in enumerate(both):
            total = s2[s].astype(F32) + r2[s].astype(F32)
            solved = jnp.where(lane + r * WC < counts[0, s], total, 0.0).astype(BF16)
            y[s] = solved
            upd[:, h * PR:(h + 1) * PR] = dot_nt(solved, panel[s]).astype(BF16)
        for s in both:
            out = pltpu.make_async_copy(y.at[s], yleaf_h.at[0, s], y_sem.at[s])
            if i < NODES // 2 - 1:
                out.start()
            outs.append(out)
        if i < NODES // 2 - 1:
            if i == 0:
                acc[7 - 7 * base] = jnp.zeros((B, TILE), F32)
            for t in range(ROOT // TILE - 1):
                got = dot_nn(upd[...], hot[i, t + base])
                acc[t + base] = got if i == 0 else acc[t + base] + got
        else:
            heard(1, 1)
            swaps = []
            for j in range(4):
                t = 2 * j + 1 - k
                give[j] = (acc[t] + dot_nn(upd[...], hot[i, t])).astype(BF16)
                swaps.append(remote(give.at[j], take.at[j], u_s.at[j], u_r.at[j], pair[0]))
            for j in range(4):
                t = 2 * j + k
                tile = acc[t] + dot_nn(upd[...], hot[i, t])
                swaps[j].wait_recv()
                tile = (tile + take[j].astype(F32)).astype(BF16)
                for q in range(4):
                    cs[j * 4 + q] = tile[:, q * 128:(q + 1) * 128]
                for q in range(4):

                    @pl.when(spot16 == q * 4 + j)
                    def _(q=q, j=j):
                        cr[q * 4 + j] = cs[j * 4 + q]

                    @pl.when(spot16 != q * 4 + j)
                    def _(q=q, j=j):
                        remote(cs.at[j * 4 + q], cr.at[spot16], c_s.at[j * 4 + q], c_r.at[spot16], (leaf, q, j))

    for out in outs[-2:]:
        out.start()
    total = jnp.zeros((B, 128), F32)
    for slot in range(16):

        @pl.when(spot16 != slot)
        def _(slot=slot):
            describe(cs.at[0], cr.at[slot], c_s.at[0], c_r.at[slot], pair[0]).wait_recv()

        total = total + cr[slot].astype(F32)
    zs[...] = total.astype(BF16)

    def to_plane(to):
        return describe(zs, zr.at[z], z_s.at[to], z_r.at[z], (to * 2 + k, r, c))

    for to in range(8):

        @pl.when((to >= group) & (to != z))
        def _(to=to):
            to_plane(to).start()

    spot = red.at[group, :, pl.ds(pl.multiple_of(r * 128, 128), 128)]

    def to_peer(shift):
        j = shift[0] * 16 + shift[1] * 4 + shift[2]
        return describe(spot, spot, g_s.at[j], g_r.at[group * 4 + r], plane(*shift))

    loads["rroot"].wait()

    @pl.when(z >= group)
    def _():
        zr[z] = zs[...]
        total = rroot[:, pl.ds(pl.multiple_of((k * 4 + r) * 128, 128), 128)].astype(F32)
        for other in range(8):

            @pl.when(z != other)
            def _(other=other):
                describe(zs, zr.at[other], z_s.at[other], z_r.at[other], pair[0]).wait_recv()

        for other in range(8):
            total = total - zr[other].astype(F32)
        spot[...] = total.astype(BF16)
        for shift in shifts[:-1]:
            to_peer(shift).start()

    loads["droot"].wait()
    for g in range(8):

        @pl.when(z >= g)
        def _(g=g):
            for q in range(4):

                @pl.when((group != g) | (r != q))
                def _(q=q):
                    block = red.at[g, :, q * 128:(q + 1) * 128]
                    describe(block, block, g_s.at[0], g_r.at[g * 4 + q], pair[0]).wait_recv()

            share = dot_nt(red[g], droot[:, g * 512:(g + 1) * 512])
            root[...] = share if g == 0 else root[...] + share

    yroot_o[...] = root[...].astype(BF16)
    for j in range(4):
        for q in range(4):

            @pl.when(spot16 != q * 4 + j)
            def _(p=j * 4 + q):
                describe(cs.at[p], cr.at[spot16], c_s.at[p], c_r.at[spot16], pair[0]).wait_send()

    for to in range(8):

        @pl.when((to >= group) & (to != z))
        def _(to=to):
            to_plane(to).wait_send()

    @pl.when(z >= group)
    def _():
        for shift in shifts[:-1]:
            to_peer(shift).wait_send()

    for copies in (first.values(), second.values(), swaps):
        for copy in copies:
            copy.wait_send()
    for out in outs:
        out.wait()


def store(y, root, y_out, root_out, y_v, root_v, sem):
    copies = [pltpu.make_async_copy(root, root_v, sem.at[0])]
    outs = [pltpu.make_async_copy(root_v, root_out, sem.at[1])]
    for i in range(NODES):
        copies.append(pltpu.make_async_copy(y.at[0, i], y_v.at[i], sem.at[2 + i]))
        outs.append(pltpu.make_async_copy(y_v.at[i], y_out.at[0, i], sem.at[10 + i]))
    for copy in copies:
        copy.start()
    for copy, out in zip(copies, outs):
        copy.wait()
        out.start()
    for out in outs:
        out.wait()


def local(rhs_leaf, dinv_leaf, panel_leaf, counts, row_index, rhs_root, dinv_root):
    anywhere = pl.BlockSpec(memory_space=pl.ANY)
    dma = pltpu.SemaphoreType.DMA
    y_leaf, y_root = pl.pallas_call(
        body,
        out_shape=(jax.ShapeDtypeStruct((1, NODES, B, WC), BF16), jax.ShapeDtypeStruct((B, 64), BF16)),
        in_specs=[anywhere] * 7,
        out_specs=(anywhere, pl.BlockSpec(memory_space=pltpu.VMEM)),
        scratch_shapes=[
            pltpu.SMEM((1, NODES), jnp.int32),
            pltpu.VMEM((NODES, B, WC), BF16),
            pltpu.VMEM((NODES, WC, WC), BF16),
            pltpu.VMEM((NODES, PR, WC), BF16),
            pltpu.VMEM((NODES, PR), jnp.int32),
            pltpu.VMEM((B, 1024), BF16),
            pltpu.VMEM((64, ROOT), BF16),
            pltpu.VMEM((NODES, B, WC), BF16),
            pltpu.VMEM((NODES, B, WC), BF16),
            pltpu.VMEM((NODES, B, WC), BF16),
            pltpu.VMEM((NODES, B, WC), BF16),
            pltpu.VMEM((NODES, B, WC), BF16),
            pltpu.VMEM((2, PR, 128), jnp.int32),
            pltpu.VMEM((NODES // 2, ROOT // TILE, 2 * PR, TILE), BF16),
            pltpu.VMEM((B, 2 * PR), BF16),
            pltpu.VMEM((ROOT // TILE, B, TILE), F32),
            pltpu.VMEM((4, B, TILE), BF16),
            pltpu.VMEM((4, B, TILE), BF16),
            pltpu.VMEM((16, B, 128), BF16),
            pltpu.VMEM((16, B, 128), BF16),
            pltpu.VMEM((B, 128), BF16),
            pltpu.VMEM((8, B, 128), BF16),
            pltpu.VMEM((8, B, 512), BF16),
            pltpu.VMEM((B, 64), F32),
            dma((28,)), dma((8,)), dma((8,)), dma((8,)), dma((8,)), dma((8,)),
            dma((16,)), dma((16,)), dma((8,)), dma((8,)), dma((32,)), dma((32,)), dma((4,)), dma((4,)),
            pltpu.SemaphoreType.REGULAR((5,)),
        ],
        compiler_params=pltpu.CompilerParams(
            collective_id=0, has_side_effects=True, vmem_limit_bytes=60 * 1024 * 1024),
        name="substitute",
    )(counts, rhs_leaf, dinv_leaf, panel_leaf, row_index, rhs_root, dinv_root)
    return pl.pallas_call(
        store,
        out_shape=(jax.ShapeDtypeStruct((1, NODES, B, WC), BF16), jax.ShapeDtypeStruct((B, 64), BF16)),
        in_specs=[anywhere] * 2,
        out_specs=(anywhere, anywhere),
        scratch_shapes=[pltpu.VMEM((NODES, B, WC), BF16), pltpu.VMEM((B, 64), BF16), dma((18,))],
        compiler_params=pltpu.CompilerParams(vmem_limit_bytes=60 * 1024 * 1024),
        name="store",
    )(y_leaf, y_root)


def solution(mesh):
    in_specs = (
        P("leaf", None, None, "col"),
        P("leaf", None, "row", "col"),
        P("leaf", None, "col", "row"),
        P("leaf", None),
        P("leaf", None, None),
        P(None, "col"),
        P(("leaf", "row"), None),
    )
    out_specs = (P("leaf", None, None, "row"), P(None, ("leaf", "row")))
    return jax.shard_map(local, mesh=mesh, in_specs=in_specs, out_specs=out_specs, check_vma=False)
```

```python
import jax
import jax.numpy as jnp
from jax import lax
from jax.experimental import pallas as pl
from jax.experimental.pallas import tpu as pltpu
from jax.sharding import PartitionSpec as P

BF16 = jnp.bfloat16
F32 = jnp.float32
MESH = pl.DeviceIdType.MESH
NODES, B, WC, PR, ROOT = 8, 64, 512, 256, 4096
TILE = 512


def dot_nn(a, b):
    return lax.dot_general(a, b, (((1,), (0,)), ((), ())), preferred_element_type=F32)


def dot_nt(a, b):
    return lax.dot_general(a, b, (((1,), (1,)), ((), ())), preferred_element_type=F32)


def body(counts_h, rhs_h, dinv_h, panel_h, rows_h, rroot_h, droot_h, yleaf_h, yroot_o,
         counts, rhs, dinv, panel, rows, rroot, droot, s1, r1, s2, r2, y, wanted, hot, upd, acc, give, take,
         cs, cr, zs, zr, red, root, in_sem, s1_s, s1_r, s2_s, s2_r, y_sem,
         c_s, c_r, z_s, z_r, g_s, g_r, u_s, u_r, relay):
    leaf, r, c = lax.axis_index("leaf"), lax.axis_index("row"), lax.axis_index("col")
    z, k = leaf // 2, leaf % 2
    near = c + 1 - 2 * (c % 2)
    far = 3 - c

    def load(src, dst, i):
        copy = pltpu.make_async_copy(src, dst, in_sem.at[i])
        copy.start()
        return copy

    order = [s for i in range(NODES // 2) for s in (i, i + NODES // 2)]
    loads = {}
    loads["counts"] = load(counts_h, counts, 0)
    for s in order:
        loads["r", s] = load(rhs_h.at[0, s], rhs.at[s], 20 + s)
        loads["d", s] = load(dinv_h.at[0, s], dinv.at[s], 1 + s)
    def plane(dk, dr, dc):
        return (z * 2 + (k + dk) % 2, (r + dr) % 4, (c + dc) % 4)

    spot16 = r * 4 + c
    group = c * 2 + k
    early = [(1, dr, 0) for dr in (2, 1, 3, 0)]
    others = [(dk, dr, dc) for dc in (2, 1, 3, 0) for dr in (2, 1, 3, 0) for dk in (1, 0)]
    shifts = early + [shift for shift in others if shift not in early and any(shift)]
    line_y = [plane(0, 0, dc) for dc in (1, 2, 3)]
    line_x = [plane(0, dr, 0) for dr in (1, 2, 3)]
    line_z = [(((z + dz) % 8) * 2 + k, r, c) for dz in (1, 7)]
    pair = [plane(1, 0, 0)]
    barrier = pltpu.get_barrier_semaphore()
    for where in line_y + line_x + pair + line_z:
        pl.semaphore_signal(barrier, inc=1, device_id=where, device_id_type=MESH)

    cut = pl.multiple_of(c * PR, PR)
    loads["rows"] = load(rows_h.at[0, :, pl.ds(cut, PR)], rows, 17)
    for s in order:
        loads["p", s] = load(panel_h.at[0, s], panel.at[s], 9 + s)
    loads["rroot"] = load(rroot_h, rroot, 18)
    loads["droot"] = load(droot_h, droot, 19)

    def tell(i, peers):
        for where in peers:
            pl.semaphore_signal(relay.at[i], inc=1, device_id=where, device_id_type=MESH)

    def heard(i, count):
        pl.semaphore_wait(relay.at[i], count)

    def describe(src, dst, ss, rs, where):
        return pltpu.make_async_remote_copy(
            src_ref=src, dst_ref=dst, send_sem=ss, recv_sem=rs, device_id=where, device_id_type=MESH)

    def remote(src, dst, ss, rs, where):
        copy = describe(src, dst, ss, rs, where)
        copy.start()
        return copy

    lane = lax.broadcasted_iota(jnp.int32, (B, WC), 1)
    first, second = {}, {}
    loads["counts"].wait()
    for i in range(NODES // 2):
        both = (i, i + NODES // 2)
        for s in both:
            loads["r", s].wait()
            loads["d", s].wait()
        for s in both:
            masked = jnp.where(lane + c * WC < counts[0, s], rhs[s].astype(F32), 0.0).astype(BF16)
            s1[s] = dot_nt(masked, dinv[s]).astype(BF16)
        if i == 0:
            pl.semaphore_wait(barrier, 9)
        for s, to in zip(both, (near, far)):
            first[s] = remote(s1.at[s], r1.at[s], s1_s.at[s], s1_r.at[s], (leaf, r, to))
        if i == 0:
            tell(0, line_x)
            tell(2, line_z)
    loads["rows"].wait()
    targets = jnp.transpose(rows[...])
    lanes = lax.broadcasted_iota(jnp.int32, (PR, 128), 1)
    for i in range(NODES // 2):
        for h in range(2):
            node = i + h * NODES // 2
            wanted[h] = jnp.broadcast_to(targets[:, node:node + 1], (PR, 128)) - lanes

        def make(t, _, i=i):
            for h in range(2):
                want = wanted[h]
                for q in range(4):
                    hot[i, t, h * PR:(h + 1) * PR, q * 128:(q + 1) * 128] = jnp.where(
                        want == t * TILE + q * 128, 1.0, 0.0).astype(BF16)
            return 0

        lax.fori_loop(0, ROOT // TILE, make, 0)
        both = (i, i + NODES // 2)
        for s in both:
            first[s].wait_recv()
        for s in both:
            s2[s] = (s1[s].astype(F32) + r1[s].astype(F32)).astype(BF16)
        for s, to in zip(both, (far, near)):
            second[s] = remote(s2.at[s], r2.at[s], s2_s.at[s], s2_r.at[s], (leaf, r, to))
        if i == 0:
            heard(0, 3)
            tell(1, pair)
        if i < 3:
            heard(2 + i, 2)
        if i < 2:
            tell(3 + i, line_z)
    for s in order:
        loads["p", s].wait()
    base = c // 2
    outs = []
    for i in range(NODES // 2):
        both = (i, i + NODES // 2)
        for s in both:
            second[s].wait_recv()
        for h, s in enumerate(both):
            total = s2[s].astype(F32) + r2[s].astype(F32)
            solved = jnp.where(lane + r * WC < counts[0, s], total, 0.0).astype(BF16)
            y[s] = solved
            upd[:, h * PR:(h + 1) * PR] = dot_nt(solved, panel[s]).astype(BF16)
        for s in both:
            out = pltpu.make_async_copy(y.at[s], yleaf_h.at[0, s], y_sem.at[s])
            if i < NODES // 2 - 1:
                out.start()
            outs.append(out)
        if i < NODES // 2 - 1:
            if i == 0:
                acc[7 - 7 * base] = jnp.zeros((B, TILE), F32)
            for t in range(ROOT // TILE - 1):
                got = dot_nn(upd[...], hot[i, t + base])
                acc[t + base] = got if i == 0 else acc[t + base] + got
        else:
            heard(1, 1)
            swaps = []
            for j in range(4):
                t = 2 * j + 1 - k
                give[j] = (acc[t] + dot_nn(upd[...], hot[i, t])).astype(BF16)
                swaps.append(remote(give.at[j], take.at[j], u_s.at[j], u_r.at[j], pair[0]))
            for j in range(4):
                t = 2 * j + k
                tile = acc[t] + dot_nn(upd[...], hot[i, t])
                swaps[j].wait_recv()
                tile = (tile + take[j].astype(F32)).astype(BF16)
                for q in range(4):
                    cs[j * 4 + q] = tile[:, q * 128:(q + 1) * 128]
                for q in range(4):

                    @pl.when(spot16 == q * 4 + j)
                    def _(q=q, j=j):
                        cr[q * 4 + j] = cs[j * 4 + q]

                    @pl.when(spot16 != q * 4 + j)
                    def _(q=q, j=j):
                        remote(cs.at[j * 4 + q], cr.at[spot16], c_s.at[j * 4 + q], c_r.at[spot16], (leaf, q, j))

    for out in outs[-2:]:
        out.start()
    total = jnp.zeros((B, 128), F32)
    for slot in range(16):

        @pl.when(spot16 != slot)
        def _(slot=slot):
            describe(cs.at[0], cr.at[slot], c_s.at[0], c_r.at[slot], pair[0]).wait_recv()

        total = total + cr[slot].astype(F32)
    zs[...] = total.astype(BF16)

    def to_plane(to):
        return describe(zs, zr.at[z], z_s.at[to], z_r.at[z], (to * 2 + k, r, c))

    for to in range(8):

        @pl.when((to >= group) & (to != z))
        def _(to=to):
            to_plane(to).start()

    spot = red.at[group, :, pl.ds(pl.multiple_of(r * 128, 128), 128)]

    def to_peer(shift):
        j = shift[0] * 16 + shift[1] * 4 + shift[2]
        return describe(spot, spot, g_s.at[j], g_r.at[group * 4 + r], plane(*shift))

    loads["rroot"].wait()

    @pl.when(z >= group)
    def _():
        zr[z] = zs[...]
        total = rroot[:, pl.ds(pl.multiple_of((k * 4 + r) * 128, 128), 128)].astype(F32)
        for other in range(8):

            @pl.when(z != other)
            def _(other=other):
                describe(zs, zr.at[other], z_s.at[other], z_r.at[other], pair[0]).wait_recv()

        for other in range(8):
            total = total - zr[other].astype(F32)
        spot[...] = total.astype(BF16)
        for shift in shifts:
            to_peer(shift).start()

    loads["droot"].wait()
    for g in range(8):

        @pl.when(z >= g)
        def _(g=g):
            for q in range(4):

                @pl.when((group != g) | (r != q))
                def _(q=q):
                    block = red.at[g, :, q * 128:(q + 1) * 128]
                    describe(block, block, g_s.at[0], g_r.at[g * 4 + q], pair[0]).wait_recv()

            share = dot_nt(red[g], droot[:, g * 512:(g + 1) * 512])
            root[...] = share if g == 0 else root[...] + share

    yroot_o[...] = root[...].astype(BF16)
    for j in range(4):
        for q in range(4):

            @pl.when(spot16 != q * 4 + j)
            def _(p=j * 4 + q):
                describe(cs.at[p], cr.at[spot16], c_s.at[p], c_r.at[spot16], pair[0]).wait_send()

    for to in range(8):

        @pl.when((to >= group) & (to != z))
        def _(to=to):
            to_plane(to).wait_send()

    @pl.when(z >= group)
    def _():
        for shift in shifts:
            to_peer(shift).wait_send()

    for copies in (first.values(), second.values(), swaps):
        for copy in copies:
            copy.wait_send()
    for out in outs:
        out.wait()


def store(y, root, y_out, root_out, y_v, root_v, sem):
    copies = [pltpu.make_async_copy(root, root_v, sem.at[0])]
    outs = [pltpu.make_async_copy(root_v, root_out, sem.at[1])]
    for i in range(NODES):
        copies.append(pltpu.make_async_copy(y.at[0, i], y_v.at[i], sem.at[2 + i]))
        outs.append(pltpu.make_async_copy(y_v.at[i], y_out.at[0, i], sem.at[10 + i]))
    for copy in copies:
        copy.start()
    for copy, out in zip(copies, outs):
        copy.wait()
        out.start()
    for out in outs:
        out.wait()


def local(rhs_leaf, dinv_leaf, panel_leaf, counts, row_index, rhs_root, dinv_root):
    anywhere = pl.BlockSpec(memory_space=pl.ANY)
    dma = pltpu.SemaphoreType.DMA
    y_leaf, y_root = pl.pallas_call(
        body,
        out_shape=(jax.ShapeDtypeStruct((1, NODES, B, WC), BF16), jax.ShapeDtypeStruct((B, 64), BF16)),
        in_specs=[anywhere] * 7,
        out_specs=(anywhere, pl.BlockSpec(memory_space=pltpu.VMEM)),
        scratch_shapes=[
            pltpu.SMEM((1, NODES), jnp.int32),
            pltpu.VMEM((NODES, B, WC), BF16),
            pltpu.VMEM((NODES, WC, WC), BF16),
            pltpu.VMEM((NODES, PR, WC), BF16),
            pltpu.VMEM((NODES, PR), jnp.int32),
            pltpu.VMEM((B, 1024), BF16),
            pltpu.VMEM((64, ROOT), BF16),
            pltpu.VMEM((NODES, B, WC), BF16),
            pltpu.VMEM((NODES, B, WC), BF16),
            pltpu.VMEM((NODES, B, WC), BF16),
            pltpu.VMEM((NODES, B, WC), BF16),
            pltpu.VMEM((NODES, B, WC), BF16),
            pltpu.VMEM((2, PR, 128), jnp.int32),
            pltpu.VMEM((NODES // 2, ROOT // TILE, 2 * PR, TILE), BF16),
            pltpu.VMEM((B, 2 * PR), BF16),
            pltpu.VMEM((ROOT // TILE, B, TILE), F32),
            pltpu.VMEM((4, B, TILE), BF16),
            pltpu.VMEM((4, B, TILE), BF16),
            pltpu.VMEM((16, B, 128), BF16),
            pltpu.VMEM((16, B, 128), BF16),
            pltpu.VMEM((B, 128), BF16),
            pltpu.VMEM((8, B, 128), BF16),
            pltpu.VMEM((8, B, 512), BF16),
            pltpu.VMEM((B, 64), F32),
            dma((28,)), dma((8,)), dma((8,)), dma((8,)), dma((8,)), dma((8,)),
            dma((16,)), dma((16,)), dma((8,)), dma((8,)), dma((32,)), dma((32,)), dma((4,)), dma((4,)),
            pltpu.SemaphoreType.REGULAR((5,)),
        ],
        compiler_params=pltpu.CompilerParams(
            collective_id=0, has_side_effects=True, vmem_limit_bytes=60 * 1024 * 1024),
        name="substitute",
    )(counts, rhs_leaf, dinv_leaf, panel_leaf, row_index, rhs_root, dinv_root)
    return pl.pallas_call(
        store,
        out_shape=(jax.ShapeDtypeStruct((1, NODES, B, WC), BF16), jax.ShapeDtypeStruct((B, 64), BF16)),
        in_specs=[anywhere] * 2,
        out_specs=(anywhere, anywhere),
        scratch_shapes=[pltpu.VMEM((NODES, B, WC), BF16), pltpu.VMEM((B, 64), BF16), dma((18,))],
        compiler_params=pltpu.CompilerParams(vmem_limit_bytes=60 * 1024 * 1024),
        name="store",
    )(y_leaf, y_root)


def solution(mesh):
    in_specs = (
        P("leaf", None, None, "col"),
        P("leaf", None, "row", "col"),
        P("leaf", None, "col", "row"),
        P("leaf", None),
        P("leaf", None, None),
        P(None, "col"),
        P(("leaf", "row"), None),
    )
    out_specs = (P("leaf", None, None, "row"), P(None, ("leaf", "row")))
    return jax.shard_map(local, mesh=mesh, in_specs=in_specs, out_specs=out_specs, check_vma=False)
```
